32 devices in a mesh: band: 2 (over y), dom: 16 (over z, x, core).
Axes of the slice: x: 2, y: 2, z: 4, core: 2. Of those that a mesh axis runs over, the one named last changes fastest.
Arguments:
- states_in: float32 [128, 16384], P('band', 'dom'), may hold values from -6 to 6
- stiffness: float32 [343, 343], replicated, may hold values from -2 to 2, as said below
- cell_scale: float32 [96], P('dom'), may hold values from 0.5 to 2
- potential: float32 [16384], P('dom'), may hold values from 0 to 2
- inv_mass_sqrt: float32 [16384], P('dom'), may hold values from 0.25 to 1.75
- cell_nodes: int32 [96, 343], P('dom'), may hold values from 0 to 1151, as said below
- shared_nodes: int32 [2048], P('dom'), may hold values from 0 to 1023, as said below
Outputs:
- filtered: float32 [128, 16384], P('band', 'dom')
- margin: float32 [128, 128], P('band')
The draws below stay inside these ranges and needn't reach their ends.
Inputs may be any that keep to these rules, and one draw needn't show every extreme that they name: `stiffness`: symmetric. `cell_nodes`: in the cells of a subdomain, an entry below 1024 is one of its own nodes and an entry l of 1024 or more stands for entry l - 1024 of the next subdomain's (cyclically) shared_nodes list; every value from 0 to 1151 occurs in the subdomain's cells. `shared_nodes`: the 128 entries of each subdomain are distinct.
All inputs are finite; a program needn't handle non-finite values.
Results may differ from the reference program's by a relative error of at most 0.0001.
Values sent between devices are 32-bit elements; how exact they have to be, the bound alone decides.
A program may use at most 64 MiB of HBM per device.

```python
import math
import jax
import jax.numpy as jnp
from jax import lax

NPC = 343
BLOCK = 64
DEGREE = 3
NODES_DEV = 1024
SHARED = 128
CELLS_DEV = 6
STATES = 128
NODES = 16384
CELLS = 96
N_BAND = 2
N_DOM = 16


def draw_stiffness(key, part):
    entries = jnp.clip(jax.random.normal(key, (NPC, NPC), jnp.float32), -4.0, 4.0)
    entries = entries / jnp.sqrt(jnp.float32(NPC))
    return (entries + entries.T) / jnp.sqrt(jnp.float32(2.0))


def draw_cell_nodes(key, part):
    local_count = NODES_DEV + SHARED
    slot_count = CELLS_DEV * NPC

    def one_domain(sub_key):
        key_first, key_second, key_third = jax.random.split(sub_key, 3)
        covering = jax.random.permutation(key_first, local_count).astype(jnp.int32)
        further = jax.random.randint(key_second, (slot_count - local_count,), 0, local_count, dtype=jnp.int32)
        joined = jnp.concatenate([covering, further])
        return jax.random.permutation(key_third, joined).reshape(CELLS_DEV, NPC)
    key_list = jax.random.split(jax.random.fold_in(key, 11), N_DOM)
    return jax.vmap(one_domain)(key_list).reshape(CELLS_DEV * N_DOM, NPC).astype(jnp.int32)


def draw_shared_nodes(key, part):

    def one_domain(sub_key):
        return jax.random.permutation(sub_key, NODES_DEV)[:SHARED].astype(jnp.int32)
    key_list = jax.random.split(jax.random.fold_in(key, 23), N_DOM)
    return jax.vmap(one_domain)(key_list).reshape(SHARED * N_DOM).astype(jnp.int32)


def levels(stream_key, extent, cuts, smallest, top_value):
    factor_of = 1.0
    for axis_at, parts in cuts:
        heights = jax.random.uniform(jax.random.fold_in(jax.random.fold_in(stream_key, 6), axis_at), (parts,), jnp.float32, smallest / len(cuts), top_value / len(cuts))
        factor_of = factor_of * jnp.repeat(jnp.exp(heights), extent[axis_at] // parts).reshape((-1,) + (1,) * (len(extent) - 1 - axis_at))
    return factor_of


def gaussian(own_key, extent, width, most, shards=(), held_as=jnp.bfloat16):
    gain = levels(own_key, extent, shards, -0.22, 0.18) if shards else 1.0
    values = jax.random.normal(own_key, extent, jnp.float32) * width * gain
    return jnp.minimum(jnp.maximum(values, -most), most).astype(held_as)


def setup_inputs(seed: int = 0) -> dict:
    arg_keys = jax.random.split(jax.random.key(seed), 8)
    states_in = gaussian(arg_keys[0], (STATES, NODES), 1.0, 6.0, ((0, 2), (1, 16)), jnp.float32)
    stiffness = draw_stiffness(jax.random.fold_in(arg_keys[7], 71), 0)
    cell_scale = jnp.clip(jnp.exp(math.log(2.0) - 1.3862944 * jax.random.uniform(arg_keys[2], (CELLS,), jnp.float32) ** levels(arg_keys[2], (CELLS,), ((0, 16),), -0.2, 0.2)), 0.5, 2.0)
    potential = jnp.clip(2.0 * jax.random.uniform(arg_keys[3], (NODES,), jnp.float32) ** levels(arg_keys[3], (NODES,), ((0, 16),), -0.2, 0.2), 0.0, 2.0)
    inv_mass_sqrt = jnp.clip(1.0 + 0.15 * jax.random.normal(arg_keys[4], (NODES,), jnp.float32), 0.25, 1.75)
    cell_nodes = draw_cell_nodes(jax.random.fold_in(arg_keys[7], 71), 0)
    shared_nodes = draw_shared_nodes(jax.random.fold_in(arg_keys[7], 71), 0)
    return dict(states_in=states_in, stiffness=stiffness, cell_scale=cell_scale, potential=potential, inv_mass_sqrt=inv_mass_sqrt, cell_nodes=cell_nodes, shared_nodes=shared_nodes)


center_shift = 1.0
half_width = 4.0

def global_nodes(cell_nodes, shared_nodes):
    count = cell_nodes.shape[0]
    holder = (jnp.arange(count, dtype=jnp.int32) // CELLS_DEV)[:, None]
    follower = (holder + 1) % N_DOM
    offset = jnp.clip(cell_nodes - NODES_DEV, 0, SHARED - 1)
    remote = shared_nodes[(follower * SHARED + offset).astype(jnp.int32)]
    inside = holder * NODES_DEV + cell_nodes
    outside = follower * NODES_DEV + remote
    return jnp.where(cell_nodes < NODES_DEV, inside, outside).astype(jnp.int32)

def operate(vector, stiffness, cell_scale, potential, inv_mass_sqrt, indices):
    scaled = vector * inv_mass_sqrt[None, :]
    cellwise = scaled[:, indices]
    product = jnp.einsum('bcj,kj->bck', cellwise, stiffness, precision=lax.Precision.HIGHEST, preferred_element_type=jnp.float32)
    product = product * cell_scale[None, :, None]
    summed = jnp.zeros_like(vector).at[:, indices].add(product)
    return inv_mass_sqrt[None, :] * summed + potential[None, :] * vector

def reference(states_in, stiffness, cell_scale, potential, inv_mass_sqrt, cell_nodes, shared_nodes):
    indices = global_nodes(cell_nodes, shared_nodes)

    def apply_once(vector):
        return operate(vector, stiffness, cell_scale, potential, inv_mass_sqrt, indices)

    def filter_block(block_states):
        previous = block_states
        current = (apply_once(block_states) - center_shift * block_states) / half_width
        for degree_step in range(DEGREE - 1):
            following = 2.0 * (apply_once(current) - center_shift * current) / half_width - previous
            previous = current
            current = following
        return current
    blocks = states_in.reshape(N_BAND, BLOCK, states_in.shape[1])
    filtered = lax.map(filter_block, blocks).reshape(STATES, states_in.shape[1])
    margin = jnp.dot(filtered, filtered.T, precision=lax.Precision.HIGHEST, preferred_element_type=jnp.float32)
    margin = margin / (NODES_DEV * N_DOM)
    return (filtered, margin)
```

```python
import functools

import jax
import jax.numpy as jnp
from jax import lax
from jax.experimental import pallas as pl
from jax.experimental.pallas import tpu as pltpu
from jax.sharding import PartitionSpec as P

DEGREE = 3
CENTER = 1.0
HALF_WIDTH = 4.0
LANES = 128
F32, BF16 = jnp.float32, jnp.bfloat16


def stacked_parts(value):
    high = value.astype(BF16)
    low = (value - high.astype(F32)).astype(BF16)
    return jnp.concatenate([high, low], axis=0)


def folded(value):
    half = value.shape[0] // 2
    return value[:half] + value[half:]


def dot(a, b):
    return jnp.dot(a, b, preferred_element_type=F32)


def dot_nt(a, b):
    return lax.dot_general(a, b, (((1,), (1,)), ((), ())), preferred_element_type=F32)


def one_hot(a, b):
    return jnp.where(a == b, 1.0, 0.0).astype(F32)


def kernel(
    n_band, n_dom, inner,
    x_ref, stiff_ref, scale_ref, pot_ref, mass_ref, cells_ref, shared_ref,
    filt_ref, margin_ref,
    idx, stiff_pad, stiff_hi, stiff_lo, gather, scatter, spread, lead,
    lead_send, lead_recv, ret_send, ret_recv, last_recv, part_send, part_recv,
    uu, yy, zz, block_send, blocks, gram, gram_recv, chunk, chunk_recv, final,
    lead_sem, ret_sem, last_sem, part_sem, block_sem, gram_sem, chunk_sem, final_sem,
):
    rows, owned = x_ref.shape
    cells, npc = cells_ref.shape
    shared = shared_ref.shape[1]
    width = idx.shape[1]
    edge = 2 * shared
    outer = n_dom // inner
    band, dom = lax.axis_index("band"), lax.axis_index("dom")
    after, before = lax.rem(dom + 1, n_dom), lax.rem(dom + n_dom - 1, n_dom)
    place, line = lax.rem(dom, inner), dom // inner

    def turned(value, by, size):
        return lax.rem(value + by, size)

    def at(b, d):
        return {"band": b, "dom": d}

    barrier = pltpu.get_barrier_semaphore()
    greeted = 0
    for k in range(n_band):
        other = turned(band, k, n_band)
        opposite = turned(band, n_band - k, n_band)
        pl.semaphore_signal(barrier, inc=1, device_id=at(other, after))
        pl.semaphore_signal(barrier, inc=1, device_id=at(opposite, before))
        greeted += 2
        if k:
            pl.semaphore_signal(barrier, inc=1, device_id=at(other, dom))
            greeted += 1
    for k in range(1, inner):
        pl.semaphore_signal(
            barrier, inc=1, device_id=at(band, line * inner + turned(place, k, inner)))
        greeted += 1
    for k in range(1, outer):
        pl.semaphore_signal(
            barrier, inc=1, device_id=at(band, turned(line, k, outer) * inner + place))
        greeted += 1

    started = []

    def send(src, dst, sems, slot, device):
        copy = pltpu.make_async_remote_copy(
            src_ref=src, dst_ref=dst, send_sem=sems.at[0, slot], recv_sem=sems.at[1, slot],
            device_id=device, device_id_type=pl.DeviceIdType.MESH)
        copy.start()
        started.append(copy)
        return copy

    mass, pot = mass_ref[...], pot_ref[...]
    shared_row = shared_ref[...]
    lead[0:rows, :] = x_ref[...]
    lead[rows:rows + 8, :] = jnp.concatenate(
        [mass, pot, jnp.zeros((6, owned), F32)], axis=0)
    pick = one_hot(lax.broadcasted_iota(jnp.int32, (owned, shared), 0), shared_row)
    lead_send[...] = jnp.dot(
        lead[...], pick, precision=lax.Precision.HIGHEST, preferred_element_type=F32)
    pl.semaphore_wait(barrier, greeted)
    lead_copy = send(lead_send, lead_recv, lead_sem, 0, at(band, before))

    idx[...] = jnp.full(idx.shape, -1.0, F32)
    idx[0:cells, 0:npc] = cells_ref[...].astype(F32)
    stiff_pad[...] = jnp.zeros(stiff_pad.shape, F32)
    stiff_pad[0:npc, 0:npc] = stiff_ref[...]
    high = stiff_pad[...].astype(BF16)
    stiff_hi[...] = high
    stiff_lo[...] = (stiff_pad[...] - high.astype(F32)).astype(BF16)
    shared_f = shared_row.astype(F32)
    shared_col = jnp.broadcast_to(shared_f, (LANES, shared)).T
    for k in range(owned // LANES):
        lane = lax.broadcasted_iota(jnp.int32, (shared, LANES), 1) + k * LANES
        spread[:, k * LANES:(k + 1) * LANES] = one_hot(shared_col, lane.astype(F32)).astype(BF16)
    local = owned + shared
    node = lax.broadcasted_iota(jnp.int32, (LANES, width), 0).astype(F32)
    lane = lax.broadcasted_iota(jnp.int32, (width, LANES), 1).astype(F32)
    shared_wide = jnp.concatenate([shared_col] * (width // LANES), axis=1)
    for c in range(cells):
        slot_row = jnp.broadcast_to(idx[c:c + 1, :], (LANES, width))
        slot_col = slot_row.T
        span = slice(c * width, (c + 1) * width)
        for k in range(local // LANES):
            tile = slice(k * LANES, (k + 1) * LANES)
            gather[c, tile, :] = one_hot(node + float(k * LANES), slot_row).astype(BF16)
            scatter[span, tile] = one_hot(lane + float(k * LANES), slot_col).astype(BF16)
        gather[c, local:, :] = one_hot(shared_wide, slot_row).astype(BF16)
        scatter[span, local:] = one_hot(shared_f, slot_col).astype(BF16)

    mass_shared, pot_shared = lead_send[rows:rows + 1, :], lead_send[rows + 1:rows + 2, :]
    partial = x_ref[...]
    current_shared = lead_send[0:rows, :]
    previous, previous_shared = None, None
    returned = None
    for t in range(DEGREE):
        last = t == DEGREE - 1
        factor = (1.0 if t == 0 else 2.0) / HALF_WIDTH
        uu[...] = stacked_parts(mass * partial)
        for c in range(cells):
            yy[c] = dot(uu[...], gather[c, 0:owned, :])
        if t == 0:
            lead_copy.wait_recv()
            mass_ghost = lead_recv[rows:rows + 1, :]
            ghost = lead_recv[0:rows, :]
            fix = None
            outside = stacked_parts(
                jnp.concatenate([mass_ghost * ghost, jnp.zeros_like(ghost)], axis=1))
        else:
            ret_copy.wait_recv()
            part_copy.wait_recv()
            fix = earlier * mass_shared * ret_recv[t - 1]
            ghost = part_recv[t - 1] + earlier * mass_ghost * returned
            current_shared = part + fix
            outside = stacked_parts(
                jnp.concatenate([mass_ghost * ghost, mass_shared * fix], axis=1))
        for c in range(cells):
            y = stacked_parts(folded(yy[c] + dot(outside, gather[c, owned:, :])))
            z = folded(dot(y, stiff_hi[...])) + dot(y[0:rows], stiff_lo[...])
            zz[:, c * width:(c + 1) * width] = stacked_parts(z * scale_ref[c])
        border = folded(dot(zz[...], scatter[:, owned:]))
        returned = border[:, 0:shared]
        ret_send[t] = returned
        if last:
            last_copies = [
                send(ret_send.at[t], last_recv.at[band], last_sem, k,
                     at(turned(band, k, n_band), after))
                for k in range(n_band)]
        else:
            ret_copy = send(ret_send.at[t], ret_recv.at[t], ret_sem, t, at(band, after))
            part = factor * (
                mass_shared * border[:, shared:] + (pot_shared - CENTER) * current_shared)
            if t:
                part = part - previous_shared
            part_send[t] = part
            part_copy = send(part_send.at[t], part_recv.at[t], part_sem, t, at(band, before))
        current = partial
        if t:
            current = current + folded(dot(stacked_parts(fix), spread[...]))
        sums = folded(dot(zz[...], scatter[:, 0:owned]))
        partial = factor * (mass * sums + (pot - CENTER) * current)
        if t:
            partial = partial - previous
        previous, previous_shared = current, current_shared
        earlier = factor

    block_send[...] = partial
    blocks[band] = partial
    block_copies = [
        send(block_send, blocks.at[band], block_sem, k - 1, at(turned(band, k, n_band), dom))
        for k in range(1, n_band)]
    for copy in last_copies:
        copy.wait_recv()
    for copy in block_copies:
        copy.wait_recv()
    for b in range(n_band):
        fix = stacked_parts(earlier * mass_shared * last_recv[b])
        blocks[b] = blocks[b] + folded(dot(fix, spread[...]))
    filtered = blocks[band]
    filt_ref[...] = filtered
    mine = stacked_parts(filtered)
    depth = rows // inner
    pieces = []
    for b in range(n_band):
        theirs = stacked_parts(blocks[b])
        pieces.append(folded(dot_nt(mine, theirs[0:rows])) + dot_nt(mine[0:rows], theirs[rows:]))
    product = jnp.concatenate(pieces, axis=1) * (1.0 / (owned * n_dom))
    for k in range(inner):
        gram[k] = product[k * depth:(k + 1) * depth]
    copies = []
    for k in range(1, inner):
        to = turned(place, k, inner)
        copies.append(send(
            gram.at[to], gram_recv.at[place], gram_sem, k - 1, at(band, line * inner + to)))
    gram_recv[place] = gram[place]
    for copy in copies:
        copy.wait_recv()
    total = gram_recv[0]
    for k in range(1, inner):
        total = total + gram_recv[k]
    chunk[...] = total
    copies = [
        send(chunk, chunk_recv.at[line], chunk_sem, k - 1,
             at(band, turned(line, k, outer) * inner + place))
        for k in range(1, outer)]
    chunk_recv[line] = total
    for copy in copies:
        copy.wait_recv()
    total = chunk_recv[0]
    for k in range(1, outer):
        total = total + chunk_recv[k]
    gram_out = final.at[place]
    gram_out[...] = total
    copies = [
        send(final.at[place], final.at[place], final_sem, k - 1,
             at(band, line * inner + turned(place, k, inner)))
        for k in range(1, inner)]
    for copy in copies:
        copy.wait_recv()
    for k in range(inner):
        margin_ref[k * depth:(k + 1) * depth, :] = final[k]
    for copy in started:
        copy.wait_send()


def rounded_up(value):
    return -(-value // LANES) * LANES


def per_device(
    n_band, n_dom,
    states_in, stiffness, cell_scale, potential, inv_mass_sqrt, cell_nodes, shared_nodes
):
    rows, owned = states_in.shape
    cells, npc = cell_nodes.shape
    shared = shared_nodes.shape[0]
    width = rounded_up(npc)
    nodes = owned + 2 * shared
    states = n_band * rows
    inner = 1
    while inner * inner * 4 <= n_dom:
        inner *= 2
    outer = n_dom // inner
    depth = rows // inner
    pairs = lambda count: pltpu.SemaphoreType.DMA((2, count))
    vmem = pltpu.VMEM
    in_vmem = pl.BlockSpec(memory_space=pltpu.VMEM)
    return pl.pallas_call(
        functools.partial(kernel, n_band, n_dom, inner),
        out_shape=(
            jax.ShapeDtypeStruct((rows, owned), F32),
            jax.ShapeDtypeStruct((rows, states), F32),
        ),
        in_specs=[in_vmem, in_vmem, pl.BlockSpec(memory_space=pltpu.SMEM)] + [in_vmem] * 4,
        out_specs=(in_vmem, in_vmem),
        scratch_shapes=[
            vmem((-(-cells // 8) * 8, width), F32),
            vmem((width, width), F32),
            vmem((width, width), BF16),
            vmem((width, width), BF16),
            vmem((cells, nodes, width), BF16),
            vmem((cells * width, nodes), BF16),
            vmem((shared, owned), BF16),
            vmem((rows + 8, owned), F32),
            vmem((rows + 8, shared), F32),
            vmem((rows + 8, shared), F32),
            vmem((DEGREE, rows, shared), F32),
            vmem((DEGREE - 1, rows, shared), F32),
            vmem((n_band, rows, shared), F32),
            vmem((DEGREE - 1, rows, shared), F32),
            vmem((DEGREE - 1, rows, shared), F32),
            vmem((2 * rows, owned), BF16),
            vmem((cells, 2 * rows, width), F32),
            vmem((2 * rows, cells * width), BF16),
            vmem((rows, owned), F32),
            vmem((n_band, rows, owned), F32),
            vmem((inner, depth, states), F32),
            vmem((inner, depth, states), F32),
            vmem((depth, states), F32),
            vmem((outer, depth, states), F32),
            vmem((inner, depth, states), F32),
            pairs(1),
            pairs(DEGREE - 1),
            pairs(n_band),
            pairs(DEGREE - 1),
            pairs(max(n_band - 1, 1)),
            pairs(max(inner - 1, 1)),
            pairs(max(outer - 1, 1)),
            pairs(max(inner - 1, 1)),
        ],
        compiler_params=pltpu.CompilerParams(collective_id=0, has_side_effects=True),
    )(
        states_in, stiffness, cell_scale, potential[None, :], inv_mass_sqrt[None, :],
        cell_nodes, shared_nodes[None, :],
    )


def solution(mesh):
    n_band, n_dom = mesh.shape["band"], mesh.shape["dom"]
    return jax.shard_map(
        functools.partial(per_device, n_band, n_dom),
        mesh=mesh,
        in_specs=(P("band", "dom"), P(), P("dom"), P("dom"), P("dom"), P("dom", None), P("dom")),
        out_specs=(P("band", "dom"), P("band", None)),
        check_vma=False,
    )
```

```python
import functools

import jax
import jax.numpy as jnp
from jax import lax
from jax.experimental import pallas as pl
from jax.experimental.pallas import tpu as pltpu
from jax.sharding import PartitionSpec as P

DEGREE = 3
CENTER = 1.0
HALF_WIDTH = 4.0
LANES = 128
F32, BF16 = jnp.float32, jnp.bfloat16


def stacked_parts(value):
    high = value.astype(BF16)
    low = (value - high.astype(F32)).astype(BF16)
    return jnp.concatenate([high, low], axis=0)


def folded(value):
    half = value.shape[0] // 2
    return value[:half] + value[half:]


def dot(a, b):
    return jnp.dot(a, b, preferred_element_type=F32)


def dot_nt(a, b):
    return lax.dot_general(a, b, (((1,), (1,)), ((), ())), preferred_element_type=F32)


def one_hot(a, b):
    return jnp.where(a == b, 1.0, 0.0).astype(F32)


def kernel(
    n_band, n_dom, inner,
    x_hbm, stiff_hbm, scale_hbm, pot_hbm, mass_hbm, cells_hbm, shared_hbm,
    filt_ref, margin_ref,
    x_ref, stiff_ref, scale_ref, pot_ref, mass_ref, cells_ref, shared_ref, load_sem,
    idx, stiff_pad, stiff_hi, stiff_lo, gather, scatter, spread, lead,
    lead_send, lead_recv, ret_send, ret_recv, last_recv, part_send, part_recv,
    uu, yy, zz, block_send, blocks, gram, gram_recv, chunk, chunk_recv, final,
    lead_sem, ret_sem, last_sem, part_sem, block_sem, gram_sem, chunk_sem, final_sem,
):
    rows, owned = x_ref.shape
    cells, npc = cells_ref.shape
    shared = shared_ref.shape[1]
    width = idx.shape[1]
    edge = 2 * shared
    outer = n_dom // inner
    band, dom = lax.axis_index("band"), lax.axis_index("dom")
    after, before = lax.rem(dom + 1, n_dom), lax.rem(dom + n_dom - 1, n_dom)
    place, line = lax.rem(dom, inner), dom // inner

    def turned(value, by, size):
        return lax.rem(value + by, size)

    def at(b, d):
        return {"band": b, "dom": d}

    pairs = (
        (shared_hbm, shared_ref), (mass_hbm, mass_ref), (pot_hbm, pot_ref), (x_hbm, x_ref),
        (cells_hbm, cells_ref), (stiff_hbm, stiff_ref), (scale_hbm, scale_ref))
    loads = [pltpu.make_async_copy(src, dst, load_sem.at[k]) for k, (src, dst) in enumerate(pairs)]
    first_loads, later_loads = loads[:4], loads[4:]
    barrier = pltpu.get_barrier_semaphore()
    greeted = 0
    for k in range(n_band):
        other = turned(band, k, n_band)
        opposite = turned(band, n_band - k, n_band)
        pl.semaphore_signal(barrier, inc=1, device_id=at(other, after))
        pl.semaphore_signal(barrier, inc=1, device_id=at(opposite, before))
        greeted += 2
        if k:
            pl.semaphore_signal(barrier, inc=1, device_id=at(other, dom))
            greeted += 1
    for k in range(1, inner):
        pl.semaphore_signal(
            barrier, inc=1, device_id=at(band, line * inner + turned(place, k, inner)))
        greeted += 1
    for k in range(1, outer):
        pl.semaphore_signal(
            barrier, inc=1, device_id=at(band, turned(line, k, outer) * inner + place))
        greeted += 1

    for load in loads:
        load.start()
    started = []

    def send(src, dst, sems, slot, device):
        copy = pltpu.make_async_remote_copy(
            src_ref=src, dst_ref=dst, send_sem=sems.at[0, slot], recv_sem=sems.at[1, slot],
            device_id=device, device_id_type=pl.DeviceIdType.MESH)
        copy.start()
        started.append(copy)
        return copy

    for load in first_loads:
        load.wait()
    mass, pot = mass_ref[...], pot_ref[...]
    shared_row = shared_ref[...]
    lead[0:rows, :] = x_ref[...]
    lead[rows:rows + 8, :] = jnp.concatenate(
        [mass, pot, jnp.zeros((6, owned), F32)], axis=0)
    pick = one_hot(lax.broadcasted_iota(jnp.int32, (owned, shared), 0), shared_row)
    lead_send[...] = jnp.dot(
        lead[...], pick, precision=lax.Precision.HIGHEST, preferred_element_type=F32)
    pl.semaphore_wait(barrier, greeted)
    lead_copy = send(lead_send, lead_recv, lead_sem, 0, at(band, before))

    for load in later_loads:
        load.wait()
    idx[...] = jnp.full(idx.shape, -1.0, F32)
    idx[0:cells, 0:npc] = cells_ref[...].astype(F32)
    stiff_pad[...] = jnp.zeros(stiff_pad.shape, F32)
    stiff_pad[0:npc, 0:npc] = stiff_ref[...]
    high = stiff_pad[...].astype(BF16)
    stiff_hi[...] = high
    stiff_lo[...] = (stiff_pad[...] - high.astype(F32)).astype(BF16)
    shared_f = shared_row.astype(F32)
    shared_col = jnp.broadcast_to(shared_f, (LANES, shared)).T
    for k in range(owned // LANES):
        lane = lax.broadcasted_iota(jnp.int32, (shared, LANES), 1) + k * LANES
        spread[:, k * LANES:(k + 1) * LANES] = one_hot(shared_col, lane.astype(F32)).astype(BF16)
    local = owned + shared
    node = lax.broadcasted_iota(jnp.int32, (LANES, width), 0).astype(F32)
    lane = lax.broadcasted_iota(jnp.int32, (width, LANES), 1).astype(F32)
    shared_wide = jnp.concatenate([shared_col] * (width // LANES), axis=1)
    for c in range(cells):
        slot_row = jnp.broadcast_to(idx[c:c + 1, :], (LANES, width))
        slot_col = slot_row.T
        span = slice(c * width, (c + 1) * width)
        for k in range(local // LANES):
            tile = slice(k * LANES, (k + 1) * LANES)
            gather[c, tile, :] = one_hot(node + float(k * LANES), slot_row).astype(BF16)
            scatter[span, tile] = one_hot(lane + float(k * LANES), slot_col).astype(BF16)
        gather[c, local:, :] = one_hot(shared_wide, slot_row).astype(BF16)
        scatter[span, local:] = one_hot(shared_f, slot_col).astype(BF16)

    mass_shared, pot_shared = lead_send[rows:rows + 1, :], lead_send[rows + 1:rows + 2, :]
    partial = x_ref[...]
    current_shared = lead_send[0:rows, :]
    previous, previous_shared = None, None
    returned = None
    for t in range(DEGREE):
        last = t == DEGREE - 1
        factor = (1.0 if t == 0 else 2.0) / HALF_WIDTH
        uu[...] = stacked_parts(mass * partial)
        for c in range(cells):
            yy[c] = dot(uu[...], gather[c, 0:owned, :])
        if t == 0:
            lead_copy.wait_recv()
            mass_ghost = lead_recv[rows:rows + 1, :]
            ghost = lead_recv[0:rows, :]
            fix = None
            outside = stacked_parts(
                jnp.concatenate([mass_ghost * ghost, jnp.zeros_like(ghost)], axis=1))
        else:
            ret_copy.wait_recv()
            part_copy.wait_recv()
            fix = earlier * mass_shared * ret_recv[t - 1]
            ghost = part_recv[t - 1] + earlier * mass_ghost * returned
            current_shared = part + fix
            outside = stacked_parts(
                jnp.concatenate([mass_ghost * ghost, mass_shared * fix], axis=1))
        for c in range(cells):
            y = stacked_parts(folded(yy[c] + dot(outside, gather[c, owned:, :])))
            z = folded(dot(y, stiff_hi[...])) + dot(y[0:rows], stiff_lo[...])
            zz[:, c * width:(c + 1) * width] = stacked_parts(z * scale_ref[c])
        border = folded(dot(zz[...], scatter[:, owned:]))
        returned = border[:, 0:shared]
        ret_send[t] = returned
        if last:
            last_copies = [
                send(ret_send.at[t], last_recv.at[band], last_sem, k,
                     at(turned(band, k, n_band), after))
                for k in range(n_band)]
        else:
            ret_copy = send(ret_send.at[t], ret_recv.at[t], ret_sem, t, at(band, after))
            part = factor * (
                mass_shared * border[:, shared:] + (pot_shared - CENTER) * current_shared)
            if t:
                part = part - previous_shared
            part_send[t] = part
            part_copy = send(part_send.at[t], part_recv.at[t], part_sem, t, at(band, before))
        current = partial
        if t:
            current = current + folded(dot(stacked_parts(fix), spread[...]))
        sums = folded(dot(zz[...], scatter[:, 0:owned]))
        partial = factor * (mass * sums + (pot - CENTER) * current)
        if t:
            partial = partial - previous
        previous, previous_shared = current, current_shared
        earlier = factor

    block_send[...] = partial
    blocks[band] = partial
    block_copies = [
        send(block_send, blocks.at[band], block_sem, k - 1, at(turned(band, k, n_band), dom))
        for k in range(1, n_band)]
    for copy in last_copies:
        copy.wait_recv()
    for copy in block_copies:
        copy.wait_recv()
    for b in range(n_band):
        fix = stacked_parts(earlier * mass_shared * last_recv[b])
        blocks[b] = blocks[b] + folded(dot(fix, spread[...]))
    filtered = blocks[band]
    filt_ref[...] = filtered
    mine = stacked_parts(filtered)
    depth = rows // inner
    pieces = []
    for b in range(n_band):
        theirs = stacked_parts(blocks[b])
        pieces.append(folded(dot_nt(mine, theirs[0:rows])) + dot_nt(mine[0:rows], theirs[rows:]))
    product = jnp.concatenate(pieces, axis=1) * (1.0 / (owned * n_dom))
    for k in range(inner):
        gram[k] = product[k * depth:(k + 1) * depth]
    copies = []
    for k in range(1, inner):
        to = turned(place, k, inner)
        copies.append(send(
            gram.at[to], gram_recv.at[place], gram_sem, k - 1, at(band, line * inner + to)))
    gram_recv[place] = gram[place]
    for copy in copies:
        copy.wait_recv()
    total = gram_recv[0]
    for k in range(1, inner):
        total = total + gram_recv[k]
    chunk[...] = total
    copies = [
        send(chunk, chunk_recv.at[line], chunk_sem, k - 1,
             at(band, turned(line, k, outer) * inner + place))
        for k in range(1, outer)]
    chunk_recv[line] = total
    for copy in copies:
        copy.wait_recv()
    total = chunk_recv[0]
    for k in range(1, outer):
        total = total + chunk_recv[k]
    gram_out = final.at[place]
    gram_out[...] = total
    copies = [
        send(final.at[place], final.at[place], final_sem, k - 1,
             at(band, line * inner + turned(place, k, inner)))
        for k in range(1, inner)]
    for copy in copies:
        copy.wait_recv()
    for k in range(inner):
        margin_ref[k * depth:(k + 1) * depth, :] = final[k]
    for copy in started:
        copy.wait_send()


def rounded_up(value):
    return -(-value // LANES) * LANES


def per_device(
    n_band, n_dom,
    states_in, stiffness, cell_scale, potential, inv_mass_sqrt, cell_nodes, shared_nodes
):
    rows, owned = states_in.shape
    cells, npc = cell_nodes.shape
    shared = shared_nodes.shape[0]
    width = rounded_up(npc)
    nodes = owned + 2 * shared
    states = n_band * rows
    inner = 1
    while inner * inner * 4 <= n_dom:
        inner *= 2
    outer = n_dom // inner
    depth = rows // inner
    pairs = lambda count: pltpu.SemaphoreType.DMA((2, count))
    vmem = pltpu.VMEM
    in_vmem = pl.BlockSpec(memory_space=pltpu.VMEM)
    return pl.pallas_call(
        functools.partial(kernel, n_band, n_dom, inner),
        out_shape=(
            jax.ShapeDtypeStruct((rows, owned), F32),
            jax.ShapeDtypeStruct((rows, states), F32),
        ),
        in_specs=[pl.BlockSpec(memory_space=pltpu.HBM)] * 7,
        out_specs=(in_vmem, in_vmem),
        scratch_shapes=[
            vmem((rows, owned), F32),
            vmem((npc, npc), F32),
            pltpu.SMEM((cells,), F32),
            vmem((1, owned), F32),
            vmem((1, owned), F32),
            vmem((cells, npc), jnp.int32),
            vmem((1, shared), jnp.int32),
            pltpu.SemaphoreType.DMA((7,)),
            vmem((-(-cells // 8) * 8, width), F32),
            vmem((width, width), F32),
            vmem((width, width), BF16),
            vmem((width, width), BF16),
            vmem((cells, nodes, width), BF16),
            vmem((cells * width, nodes), BF16),
            vmem((shared, owned), BF16),
            vmem((rows + 8, owned), F32),
            vmem((rows + 8, shared), F32),
            vmem((rows + 8, shared), F32),
            vmem((DEGREE, rows, shared), F32),
            vmem((DEGREE - 1, rows, shared), F32),
            vmem((n_band, rows, shared), F32),
            vmem((DEGREE - 1, rows, shared), F32),
            vmem((DEGREE - 1, rows, shared), F32),
            vmem((2 * rows, owned), BF16),
            vmem((cells, 2 * rows, width), F32),
            vmem((2 * rows, cells * width), BF16),
            vmem((rows, owned), F32),
            vmem((n_band, rows, owned), F32),
            vmem((inner, depth, states), F32),
            vmem((inner, depth, states), F32),
            vmem((depth, states), F32),
            vmem((outer, depth, states), F32),
            vmem((inner, depth, states), F32),
            pairs(1),
            pairs(DEGREE - 1),
            pairs(n_band),
            pairs(DEGREE - 1),
            pairs(max(n_band - 1, 1)),
            pairs(max(inner - 1, 1)),
            pairs(max(outer - 1, 1)),
            pairs(max(inner - 1, 1)),
        ],
        compiler_params=pltpu.CompilerParams(collective_id=0, has_side_effects=True, vmem_limit_bytes=28 << 20),
    )(*[pltpu.with_memory_space_constraint(value, pltpu.HBM) for value in (
        states_in, stiffness, cell_scale, potential[None, :], inv_mass_sqrt[None, :],
        cell_nodes, shared_nodes[None, :],
    )])


def solution(mesh):
    n_band, n_dom = mesh.shape["band"], mesh.shape["dom"]
    return jax.shard_map(
        functools.partial(per_device, n_band, n_dom),
        mesh=mesh,
        in_specs=(P("band", "dom"), P(), P("dom"), P("dom"), P("dom"), P("dom", None), P("dom")),
        out_specs=(P("band", "dom"), P("band", None)),
        check_vma=False,
    )
```
